32 devices in a mesh: group: 2 (over y), gx: 4 (over z), gy: 2 (over x), sec: 2 (over core).
Axes of the slice: x: 2, y: 2, z: 4, core: 2. Of those that a mesh axis runs over, the one named last changes fastest.
Arguments:
- pressure: float32 [2, 32, 32, 128], P('sec', ('group', 'gx'), 'gy'), parts along dimension 1, may hold values from -6 to 6
- pressure_before: float32 [2, 32, 32, 128], P('sec', ('group', 'gx'), 'gy'), parts along dimension 1, may hold values from -6 to 6
- quasi: float32 [2, 32, 32, 128], P('sec', ('group', 'gx'), 'gy'), parts along dimension 1, may hold values from -6 to 6
- quasi_before: float32 [2, 32, 32, 128], P('sec', ('group', 'gx'), 'gy'), parts along dimension 1, may hold values from -6 to 6
- courant: float32 [16, 32, 128], P('gx', 'gy'), may hold values from 0.02 to 0.08
- epsilon: float32 [16, 32, 128], P('gx', 'gy'), may hold values from 0 to 0.3
- delta: float32 [16, 32, 128], P('gx', 'gy'), may hold values from -0.1 to 0.2
- tilt: float32 [16, 32, 128], P('gx', 'gy'), may hold values from -3.140625 to 3.140625
- azimuth: float32 [16, 32, 128], P('gx', 'gy'), may hold values from -3.140625 to 3.140625
- plan: int32 [4], replicated, may hold values from 1 to 8, as said below
- lags: int32 [5], replicated, may hold values from -4 to 4, as said below
Outputs:
- pressure_final: float32 [2, 32, 32, 128], P('sec', ('group', 'gx'), 'gy'), parts along dimension 1
- quasi_final: float32 [2, 32, 32, 128], P('sec', ('group', 'gx'), 'gy'), parts along dimension 1
- image: float32 [5, 32, 32, 128], P(None, ('group', 'gx'), 'gy', 'sec'), parts along dimension 1
The draws below stay inside these ranges and needn't reach their ends.
There are 2 independent parts, one for each index of `group`. The reference program is written for one: setup_inputs(seed, part) draws one part's arguments, and reference() takes and returns one part's arrays. A program takes and returns all parts, laid end to end along the dimension named above; an argument that names none is the same for every part. Nothing has to cross between parts.
Inputs may be any that keep to these rules, and one draw needn't show every extreme that they name: `plan`: distinct steps in rising order; the last entry is 8. Distinct lags; the first is -4 and the last 4.
All inputs are finite; a program needn't handle non-finite values.
Results may differ from the reference program's by a relative error of at most 0.0001.
Values sent between devices are 32-bit elements; how exact they have to be, the bound alone decides.
A program may use at most 64 MiB of HBM per device.

```python
import math
import jax
import jax.numpy as jnp
from jax import lax

NZ = 128
STEPS = 8
NSNAP = 4
HOFF = 5
LAGMAX = 4
NX = 16
NY = 32


def draw_plan(key, part):
    candidates = jnp.arange(1, STEPS, dtype=jnp.int32)
    earlier = jax.random.permutation(jax.random.fold_in(key, 11), candidates)[:NSNAP - 1]
    earlier = jnp.sort(earlier.astype(jnp.int32))
    return jnp.concatenate([earlier, jnp.full((1,), STEPS, jnp.int32)])


def draw_lags(key, part):
    middle_values = jnp.arange(-(LAGMAX - 1), LAGMAX, dtype=jnp.int32)
    chosen = jax.random.permutation(jax.random.fold_in(key, 23), middle_values)[:HOFF - 2]
    return jnp.concatenate([jnp.full((1,), -LAGMAX, jnp.int32), chosen.astype(jnp.int32), jnp.full((1,), LAGMAX, jnp.int32)])


def block_levels(key, dims, shards, low, high):
    factor_of, own = 1.0, jax.random.fold_in(key, 6)
    for position, blocks in shards:
        heights = jnp.exp(jax.random.uniform(jax.random.fold_in(own, position), (blocks,), jnp.float32, low / len(shards), high / len(shards)))
        factor_of = factor_of * jnp.repeat(heights, dims[position] // blocks).reshape([-1 if axis == position else 1 for axis in range(len(dims))])
    return factor_of


def scatter_about(rng, extent, deviation, limit, pieces=(), held_as=jnp.bfloat16):
    level = block_levels(rng, extent, pieces, -0.22, 0.18) if pieces else 1.0
    values = jax.random.normal(rng, extent, jnp.float32) * deviation * level
    return jnp.minimum(jnp.maximum(values, -limit), limit).astype(held_as)


def setup_inputs(seed: int = 0, part: int = 0) -> dict:
    key_of = jax.random.split(jax.random.key(seed), 12)
    part_keys = jax.random.split(jax.random.fold_in(key_of[11], part), 12)
    return {
        "pressure": scatter_about(part_keys[0], (2, NX, NY, NZ), 1.0, 6.0, ((0, 2), (1, 4), (2, 2)), jnp.float32),
        "pressure_before": scatter_about(part_keys[1], (2, NX, NY, NZ), 1.0, 6.0, ((0, 2), (1, 4), (2, 2)), jnp.float32),
        "quasi": scatter_about(part_keys[2], (2, NX, NY, NZ), 1.0, 6.0, ((0, 2), (1, 4), (2, 2)), jnp.float32),
        "quasi_before": scatter_about(part_keys[3], (2, NX, NY, NZ), 1.0, 6.0, ((0, 2), (1, 4), (2, 2)), jnp.float32),
        "courant": jnp.clip(jnp.exp(math.log(0.08) - 1.3862944 * jax.random.uniform(key_of[4], (NX, NY, NZ), jnp.float32) ** block_levels(key_of[4], (NX, NY, NZ), ((0, 4), (1, 2)), -0.2, 0.2)), 0.02, 0.08),
        "epsilon": jnp.clip(0.3 * jax.random.uniform(key_of[5], (NX, NY, NZ), jnp.float32) ** block_levels(key_of[5], (NX, NY, NZ), ((0, 4), (1, 2)), -0.2, 0.2), 0.0, 0.3),
        "delta": jnp.clip(-0.1 + 0.3 * jax.random.uniform(key_of[6], (NX, NY, NZ), jnp.float32) ** block_levels(key_of[6], (NX, NY, NZ), ((0, 4), (1, 2)), -0.2, 0.2), -0.1, 0.2),
        "tilt": jnp.clip(jax.random.uniform(key_of[7], (NX, NY, NZ), jnp.float32, -3.140625, 3.140625), -3.140625, 3.140625),
        "azimuth": jnp.clip(jax.random.uniform(key_of[8], (NX, NY, NZ), jnp.float32, -3.140625, 3.140625), -3.140625, 3.140625),
        "plan": draw_plan(jax.random.fold_in(key_of[11], 71), part),
        "lags": draw_lags(jax.random.fold_in(key_of[11], 71), part),
    }


SECOND = (-205.0 / 72.0, 8.0 / 5.0, -1.0 / 5.0, 8.0 / 315.0, -1.0 / 560.0)
FIRST = (4.0 / 5.0, -1.0 / 5.0, 4.0 / 105.0, -1.0 / 280.0)


def second_along(values, dimension):
    amount = values.shape[dimension] - 8
    result = SECOND[0] * lax.slice_in_dim(values, 4, 4 + amount, axis=dimension)
    for offset in range(1, 5):
        result = result + SECOND[offset] * (lax.slice_in_dim(values, 4 + offset, 4 + offset + amount, axis=dimension) + lax.slice_in_dim(values, 4 - offset, 4 - offset + amount, axis=dimension))
    return result


def first_along(values, dimension):
    amount = values.shape[dimension] - 8
    result = FIRST[0] * (lax.slice_in_dim(values, 5, 5 + amount, axis=dimension) - lax.slice_in_dim(values, 3, 3 + amount, axis=dimension))
    for offset in range(2, 5):
        result = result + FIRST[offset - 1] * (lax.slice_in_dim(values, 4 + offset, 4 + offset + amount, axis=dimension) - lax.slice_in_dim(values, 4 - offset, 4 - offset + amount, axis=dimension))
    return result


def trimmed(values, dimensions):
    for dimension in dimensions:
        values = lax.slice_in_dim(values, 4, values.shape[dimension] - 4, axis=dimension)
    return values


def orientation(tilt, azimuth):
    sin_tilt = jnp.sin(tilt)
    cos_tilt = jnp.cos(tilt)
    sin_azim = jnp.sin(azimuth)
    cos_azim = jnp.cos(azimuth)
    square_sin = sin_tilt * sin_tilt
    double_tilt = jnp.sin(2.0 * tilt)
    return (square_sin * cos_azim * cos_azim, square_sin * sin_azim * sin_azim, cos_tilt * cos_tilt,
            square_sin * jnp.sin(2.0 * azimuth), double_tilt * sin_azim, double_tilt * cos_azim)


def tilted_terms(padded, weights):
    curve_xx = trimmed(second_along(padded, 1), (2, 3))
    curve_yy = trimmed(second_along(padded, 2), (1, 3))
    curve_zz = trimmed(second_along(padded, 3), (1, 2))
    slope_x = first_along(padded, 1)
    slope_y = first_along(padded, 2)
    curve_xy = trimmed(first_along(slope_x, 2), (3,))
    curve_xz = trimmed(first_along(slope_x, 3), (2,))
    curve_yz = trimmed(first_along(slope_y, 3), (1,))
    axial = (weights[0] * curve_xx + weights[1] * curve_yy + weights[2] * curve_zz
             + weights[3] * curve_xy + weights[4] * curve_yz + weights[5] * curve_xz)
    laplace = curve_xx + curve_yy + curve_zz
    return axial, laplace


def advance(now_p, before_p, now_q, before_q, axial_p, laplace_p, axial_q, courant, epsilon, delta):
    flat_p = laplace_p - axial_p
    next_p = 2.0 * now_p - before_p + courant * ((1.0 + 2.0 * epsilon) * flat_p + axial_q)
    next_q = 2.0 * now_q - before_q + courant * ((1.0 + 2.0 * delta) * flat_p + axial_q)
    return next_p, next_q


def reference(pressure, pressure_before, quasi, quasi_before, courant, epsilon, delta, tilt, azimuth, plan, lags):
    weights = orientation(tilt, azimuth)
    snapshots = jnp.zeros((2, NSNAP, NX, NY, NZ), jnp.float32)
    for step in range(STEPS):
        stacked = jnp.concatenate([pressure, quasi], 0)
        padded = jnp.pad(stacked, ((0, 0), (4, 4), (4, 4), (4, 4)))
        axial, laplace = tilted_terms(padded, weights)
        next_p, next_q = advance(pressure, pressure_before, quasi, quasi_before,
                                 axial[0:2], laplace[0:2], axial[2:4], courant, epsilon, delta)
        pressure_before, quasi_before = pressure, quasi
        pressure, quasi = next_p, next_q
        picked = (plan == step + 1).astype(jnp.float32)
        snapshots = snapshots + picked[None, :, None, None, None] * pressure[:, None]
    padded_snaps = jnp.pad(snapshots, ((0, 0), (0, 0), (LAGMAX, LAGMAX), (0, 0), (0, 0)))
    images = []
    for offset_index in range(HOFF):
        lag_cells = lags[offset_index].astype(jnp.int32)
        source = lax.dynamic_slice_in_dim(padded_snaps[0], (LAGMAX - lag_cells).astype(jnp.int32), NX, 1)
        receiver = lax.dynamic_slice_in_dim(padded_snaps[1], (LAGMAX + lag_cells).astype(jnp.int32), NX, 1)
        images.append(jnp.sum(source * receiver, axis=0))
    return pressure, quasi, jnp.stack(images)
```

```python
import functools

import jax
import jax.numpy as jnp
from jax import lax
from jax.experimental import pallas as pl
from jax.experimental.pallas import tpu as pltpu
from jax.sharding import PartitionSpec as P

STEPS = 8
REACH = 4
LEAD = 8

SECOND = (-205.0 / 72.0, 8.0 / 5.0, -1.0 / 5.0, 8.0 / 315.0, -1.0 / 560.0)
FIRST = (4.0 / 5.0, -1.0 / 5.0, 4.0 / 105.0, -1.0 / 280.0)
MESH = pl.DeviceIdType.MESH
WAYS = ((0, -1), (0, 1), (-1, 0), (1, 0), (-1, -1), (-1, 1), (1, -1), (1, 1))


def first_of(at):
    result = FIRST[0] * (at(1) - at(-1))
    for m in range(2, 5):
        result = result + FIRST[m - 1] * (at(m) - at(-m))
    return result


def second_of(at):
    result = SECOND[0] * at(0)
    for m in range(1, 5):
        result = result + SECOND[m] * (at(m) + at(-m))
    return result


def kernel(
    shape, p_in, pb_in, q_in, qb_in, courant, epsilon, delta, tilt, azimuth, plan, lags,
    p_out, q_out, image,
    field, edge_out, edge_in, other, weight, partial, slope, send, recv, send_sec, recv_sec,
):
    nx, ny = shape
    ix, iy, sec = lax.axis_index("gx"), lax.axis_index("gy"), lax.axis_index("sec")
    X, Y, Z = p_in.shape[1:]
    rows = pl.ds(LEAD, Y)

    def exists(dx, dy):
        ok = (ix + dx >= 0) & (ix + dx < nx) & (iy + dy >= 0) & (iy + dy < ny)
        return ok

    def copy(slot, k):
        dx, dy = WAYS[k]
        if dy == 0:
            start, land = (X, 0) if dx > 0 else (REACH, X + REACH)
            src = field.at[slot, :, pl.ds(start, REACH), rows, :]
            dst = field.at[slot, :, pl.ds(land, REACH), rows, :]
        else:
            side = 0 if dy > 0 else 1
            start, land, many = {0: (0, REACH, X), 1: (X - REACH, 0, REACH), -1: (0, X + REACH, REACH)}[dx]
            src = edge_out.at[slot, side, pl.ds(start, many)]
            dst = edge_in.at[slot, side, pl.ds(land, many)]
        return pltpu.make_async_remote_copy(
            src_ref=src, dst_ref=dst, send_sem=send.at[slot, k], recv_sem=recv.at[slot, k],
            device_id={"gx": ix + dx, "gy": iy + dy}, device_id_type=MESH)

    def last_copy(k):
        dx, dy = WAYS[k]
        start, land = (X, 0) if dx > 0 else (REACH, X + REACH)
        last = STEPS + 1
        return pltpu.make_async_remote_copy(
            src_ref=field.at[last, 0, pl.ds(start, REACH), rows, :],
            dst_ref=field.at[last, 0, pl.ds(land, REACH), rows, :],
            send_sem=send.at[last, k], recv_sem=recv.at[last, k],
            device_id={"gx": ix + dx, "gy": iy}, device_id_type=MESH)

    def share(slot):
        return pltpu.make_async_remote_copy(
            src_ref=field.at[slot, 0, :, rows, :], dst_ref=other.at[slot],
            send_sem=send_sec.at[slot], recv_sem=recv_sec.at[slot],
            device_id={"sec": 1 - sec}, device_id_type=MESH)

    def start_all(slot):
        for k in (2, 3, 4, 5, 6, 7, 0, 1):
            @pl.when(exists(*WAYS[k]))
            def _():
                copy(slot, k).start()

    def await_from(slot, ks):
        for k in ks:
            dx, dy = WAYS[k]

            @pl.when(exists(-dx, -dy))
            def _():
                copy(slot, k).wait_recv()

    barrier = pltpu.get_barrier_semaphore()
    for dx, dy in WAYS:
        @pl.when(exists(dx, dy))
        def _():
            pl.semaphore_signal(barrier, inc=1, device_id={"gx": ix + dx, "gy": iy + dy}, device_id_type=MESH)
    pl.semaphore_signal(barrier, inc=1, device_id={"sec": 1 - sec}, device_id_type=MESH)

    def put_edges(slot, x, p, q):
        edge_out[slot, 0, x, 0:REACH] = q[Y - REACH:]
        edge_out[slot, 0, x, REACH:] = p[Y - REACH:]
        edge_out[slot, 1, x, 0:REACH] = p[:REACH]
        edge_out[slot, 1, x, REACH:] = q[:REACH]

    for x in range(X):
        p, q = p_in[0, x], q_in[0, x]
        field[1, 0, REACH + x, LEAD:LEAD + Y] = p
        field[1, 1, REACH + x, LEAD:LEAD + Y] = q
        put_edges(1, x, p, q)
        field[0, 0, REACH + x, LEAD:LEAD + Y] = pb_in[0, x]
        field[0, 1, REACH + x, LEAD:LEAD + Y] = qb_in[0, x]

    pl.semaphore_wait(barrier, 1 + sum(exists(*way).astype(jnp.int32) for way in WAYS))
    start_all(1)

    for beyond, at in ((ix == 0, 0), (ix == nx - 1, X + REACH)):
        @pl.when(beyond)
        def _():
            @pl.loop(1, STEPS + 2)
            def _(slot):
                field[slot, :, at:at + REACH, LEAD:LEAD + Y] = jnp.zeros((2, REACH, Y, Z), jnp.float32)
                edge_in[slot, :, at:at + REACH] = jnp.zeros((2, REACH, 8, Z), jnp.float32)
    for beyond, side in ((iy == 0, 0), (iy == ny - 1, 1)):
        @pl.when(beyond)
        def _():
            @pl.loop(1, STEPS + 2)
            def _(slot):
                edge_in[slot, side] = jnp.zeros((X + 2 * REACH, 8, Z), jnp.float32)

    for x in range(X):
        t, a, c = tilt[x], azimuth[x], courant[x]
        st, ct, sa, ca = jnp.sin(t), jnp.cos(t), jnp.sin(a), jnp.cos(a)
        square, double = st * st, 2.0 * st * ct
        weight[0, x] = square * ca * ca
        weight[1, x] = square * sa * sa
        weight[2, x] = ct * ct
        weight[3, x] = square * (2.0 * sa * ca)
        weight[4, x] = double * sa
        weight[5, x] = double * ca
        weight[6, x] = c * (1.0 + 2.0 * epsilon[x])
        weight[7, x] = c * (1.0 + 2.0 * delta[x])

    lane = lax.broadcasted_iota(jnp.int32, (Y, Z), 1)
    inside = {m: (lane + m >= 0) & (lane + m < Z) for m in range(-4, 5) if m}

    def along_z(value):
        def at(m):
            if m == 0:
                return value
            return jnp.where(inside[m], pltpu.roll(value, (-m) % Z, 1), 0.0)
        return at

    @pl.loop(1, STEPS + 1)
    def _(cur):
        def blend(f, i, x):
            w = weight[i, x]
            if f == 1:
                return w
            return 1.0 - w if i < 3 else -w

        for f in range(2):
            for x in range(X):
                value = field[cur, f, REACH + x, LEAD:LEAD + Y]
                partial[f, x] = blend(f, 2, x) * second_of(along_z(value))

        def open_edges(x):
            low, high = edge_in[cur, 0, x], edge_in[cur, 1, x]
            field[cur, 0, x, LEAD - REACH:LEAD] = low[REACH:]
            field[cur, 1, x, LEAD - REACH:LEAD] = low[:REACH]
            field[cur, 0, x, LEAD + Y:LEAD + Y + REACH] = high[:REACH]
            field[cur, 1, x, LEAD + Y:LEAD + Y + REACH] = high[REACH:]

        await_from(cur, (0, 1))
        for x in range(X):
            open_edges(REACH + x)
        for f in range(2):
            for x in range(X):
                def at_y(m):
                    return field[cur, f, REACH + x, LEAD + m:LEAD + m + Y]
                total = partial[f, x] + blend(f, 1, x) * second_of(at_y)
                partial[f, x] = total + blend(f, 4, x) * first_of(along_z(first_of(at_y)))

        await_from(cur, (2, 3, 4, 5, 6, 7))

        @pl.when(cur > 1)
        def _():
            share(cur).start()

        for x in range(REACH):
            open_edges(x)
            open_edges(X + REACH + x)
        for x in range(X):
            both = []
            for f in range(2):
                def at_x(m):
                    return field[cur, f, REACH + x + m, LEAD:LEAD + Y]

                def at_x_wide(m):
                    return field[cur, f, REACH + x + m, LEAD - REACH:LEAD + Y + REACH]
                total = partial[f, x] + blend(f, 0, x) * second_of(at_x)
                slope[f, x] = first_of(at_x_wide)
                total = total + blend(f, 5, x) * first_of(along_z(slope[f, x, REACH:REACH + Y]))
                both.append(total + blend(f, 3, x) * first_of(
                    lambda m: slope[f, x, REACH + m:REACH + m + Y]))
            h2p, h1q = both
            push = courant[x] * h1q
            p = 2.0 * field[cur, 0, REACH + x, LEAD:LEAD + Y] - field[cur - 1, 0, REACH + x, LEAD:LEAD + Y]
            q = 2.0 * field[cur, 1, REACH + x, LEAD:LEAD + Y] - field[cur - 1, 1, REACH + x, LEAD:LEAD + Y]
            p = p + (weight[6, x] * h2p + push)
            q = q + (weight[7, x] * h2p + push)
            field[cur + 1, 0, REACH + x, LEAD:LEAD + Y] = p
            field[cur + 1, 1, REACH + x, LEAD:LEAD + Y] = q
            put_edges(cur + 1, x, p, q)

        @pl.when(cur < STEPS)
        def _():
            start_all(cur + 1)

    last = STEPS + 1
    for k in (2, 3):
        @pl.when(exists(*WAYS[k]))
        def _():
            last_copy(k).start()
    for x in range(X):
        p_out[0, x] = field[last, 0, REACH + x, LEAD:LEAD + Y]
        q_out[0, x] = field[last, 1, REACH + x, LEAD:LEAD + Y]
    for k in (2, 3):
        @pl.when(exists(-WAYS[k][0], 0))
        def _():
            last_copy(k).wait_recv()
    share(last).start()

    @pl.loop(2, STEPS + 2)
    def _(slot):
        share(slot).wait_recv()

    turn = 1 - 2 * sec
    half = Z // 2
    for i in range(lags.shape[0]):
        shift = lags[i] * turn
        for x in range(X):
            total = None
            for j in range(plan.shape[0]):
                slot = plan[j] + 1
                term = field[slot, 0, REACH + x - shift, LEAD:LEAD + Y] * other[slot, REACH + x + shift]
                total = term if total is None else total + term
            image[i, x] = jnp.where(sec == 0, total, pltpu.roll(total, half, 1))[:, :half]

    @pl.loop(1, STEPS + 1)
    def _(slot):
        for k in range(len(WAYS)):
            @pl.when(exists(*WAYS[k]))
            def _():
                copy(slot, k).wait_send()
    for k in (2, 3):
        @pl.when(exists(*WAYS[k]))
        def _():
            last_copy(k).wait_send()

    @pl.loop(2, STEPS + 2)
    def _(slot):
        share(slot).wait_send()


def on_device(mesh_shape, *args):
    p, plan, lags = args[0], args[9], args[10]
    X, Y, Z = p.shape[1:]
    slots, wide = STEPS + 2, X + 2 * REACH
    dma = pltpu.SemaphoreType.DMA
    vmem, smem = pl.BlockSpec(memory_space=pltpu.VMEM), pl.BlockSpec(memory_space=pltpu.SMEM)
    return pl.pallas_call(
        functools.partial(kernel, mesh_shape),
        out_shape=(
            jax.ShapeDtypeStruct(p.shape, jnp.float32),
            jax.ShapeDtypeStruct(p.shape, jnp.float32),
            jax.ShapeDtypeStruct((lags.shape[0], X, Y, Z // 2), jnp.float32),
        ),
        in_specs=[vmem] * 9 + [smem] * 2,
        out_specs=(vmem, vmem, vmem),
        scratch_shapes=[
            pltpu.VMEM((slots, 2, wide, Y + 2 * LEAD, Z), jnp.float32),
            pltpu.VMEM((slots, 2, X, 8, Z), jnp.float32),
            pltpu.VMEM((slots, 2, wide, 8, Z), jnp.float32),
            pltpu.VMEM((slots, wide, Y, Z), jnp.float32),
            pltpu.VMEM((8, X, Y, Z), jnp.float32),
            pltpu.VMEM((2, X, Y, Z), jnp.float32),
            pltpu.VMEM((2, X, Y + 2 * REACH, Z), jnp.float32),
            dma((slots, len(WAYS))),
            dma((slots, len(WAYS))),
            dma((slots,)),
            dma((slots,)),
        ],
        compiler_params=pltpu.CompilerParams(collective_id=0, has_side_effects=True),
        name="steps",
    )(*args)


def solution(mesh):
    field, medium = P("sec", ("group", "gx"), "gy", None), P("gx", "gy", None)
    return jax.shard_map(
        functools.partial(on_device, (mesh.shape["gx"], mesh.shape["gy"])),
        mesh=mesh,
        in_specs=(field,) * 4 + (medium,) * 5 + (P(), P()),
        out_specs=(field, field, P(None, ("group", "gx"), "gy", "sec")),
        check_vma=False,
    )
```

```python
import functools

import jax
import jax.numpy as jnp
from jax import lax
from jax.experimental import pallas as pl
from jax.experimental.pallas import tpu as pltpu
from jax.sharding import PartitionSpec as P

STEPS = 8
REACH = 4
LEAD = 8
PIECE = 4

SECOND = (-205.0 / 72.0, 8.0 / 5.0, -1.0 / 5.0, 8.0 / 315.0, -1.0 / 560.0)
FIRST = (4.0 / 5.0, -1.0 / 5.0, 4.0 / 105.0, -1.0 / 280.0)
MESH = pl.DeviceIdType.MESH
WAYS = ((0, -1), (0, 1), (-1, 0), (1, 0), (-1, -1), (-1, 1), (1, -1), (1, 1))


def first_of(at):
    result = FIRST[0] * (at(1) - at(-1))
    for m in range(2, 5):
        result = result + FIRST[m - 1] * (at(m) - at(-m))
    return result


def second_of(at):
    result = SECOND[0] * at(0)
    for m in range(1, 5):
        result = result + SECOND[m] * (at(m) + at(-m))
    return result


def kernel(
    shape, p_in, pb_in, q_in, qb_in, courant, epsilon, delta, tilt, azimuth, plan, lags,
    p_out, q_out, image,
    field, edge_out, edge_in, other, weight, partial, slope, stacked, tail, send, recv, send_sec, recv_sec,
):
    nx, ny = shape
    ix, iy, sec = lax.axis_index("gx"), lax.axis_index("gy"), lax.axis_index("sec")
    X, Y, Z = p_in.shape[1:]
    rows = pl.ds(LEAD, Y)

    def exists(dx, dy):
        ok = (ix + dx >= 0) & (ix + dx < nx) & (iy + dy >= 0) & (iy + dy < ny)
        return ok

    def copy(slot, k, c):
        dx, dy = WAYS[k]
        begin, many = c * PIECE, PIECE
        if dx == 0:
            start, land, begin, many = 0, REACH, 0, X
        elif dx > 0:
            start, land = X - REACH, 0
        else:
            start, land = 0, X + REACH
        if dy == 0:
            src = field.at[slot, :, pl.ds(REACH + start + begin, many), rows, :]
            dst = field.at[slot, :, pl.ds(land + begin, many), rows, :]
        else:
            side = 0 if dy > 0 else 1
            src = edge_out.at[slot, side, pl.ds(start + begin, many)]
            dst = edge_in.at[slot, side, pl.ds(land + begin, many)]
        return pltpu.make_async_remote_copy(
            src_ref=src, dst_ref=dst, send_sem=send.at[slot, k, c], recv_sem=recv.at[slot, k, c],
            device_id={"gx": ix + dx, "gy": iy + dy}, device_id_type=MESH)

    def pieces(k):
        return range(REACH // PIECE if WAYS[k][0] else 1)

    last = STEPS + 1

    def last_copy(k, cross):
        dx = WAYS[k][0]
        start, land = (X, 0) if dx > 0 else (REACH, X + REACH)
        return pltpu.make_async_remote_copy(
            src_ref=tail.at[0, pl.ds(start, REACH)], dst_ref=tail.at[int(cross), pl.ds(land, REACH)],
            send_sem=send.at[last, k + 2 * cross, 0], recv_sem=recv.at[last, k + 2 * cross, 0],
            device_id={"gx": ix + dx, "sec": 1 - sec if cross else sec}, device_id_type=MESH)

    def share(slot):
        return pltpu.make_async_remote_copy(
            src_ref=field.at[slot, 0, :, rows, :], dst_ref=other.at[slot],
            send_sem=send_sec.at[slot], recv_sem=recv_sec.at[slot],
            device_id={"sec": 1 - sec}, device_id_type=MESH)

    def last_share():
        return pltpu.make_async_remote_copy(
            src_ref=tail.at[0, pl.ds(REACH, X)], dst_ref=tail.at[1, pl.ds(REACH, X)],
            send_sem=send_sec.at[last], recv_sem=recv_sec.at[last],
            device_id={"sec": 1 - sec}, device_id_type=MESH)

    def start_ready(slot, x):
        for k in (4, 5, 6, 7, 0, 1, 2, 3):
            dx = WAYS[k][0]
            for c in pieces(k):
                end = X - 1 if dx == 0 else (c + 1) * PIECE - 1 + (X - REACH if dx > 0 else 0)
                if end == x:
                    @pl.when(exists(*WAYS[k]))
                    def _():
                        copy(slot, k, c).start()

    def await_from(slot, ks):
        for k in ks:
            dx, dy = WAYS[k]

            @pl.when(exists(-dx, -dy))
            def _():
                for c in pieces(k):
                    copy(slot, k, c).wait_recv()

    barrier = pltpu.get_barrier_semaphore()
    for dx, dy in WAYS:
        @pl.when(exists(dx, dy))
        def _():
            pl.semaphore_signal(barrier, inc=1, device_id={"gx": ix + dx, "gy": iy + dy}, device_id_type=MESH)
    for dx in (-1, 1):
        @pl.when(exists(dx, 0))
        def _():
            pl.semaphore_signal(barrier, inc=1, device_id={"gx": ix + dx, "sec": 1 - sec}, device_id_type=MESH)
    pl.semaphore_signal(barrier, inc=1, device_id={"sec": 1 - sec}, device_id_type=MESH)

    def put_edges(slot, x, p, q):
        edge_out[slot, 0, x, 0:REACH] = q[Y - REACH:]
        edge_out[slot, 0, x, REACH:] = p[Y - REACH:]
        edge_out[slot, 1, x, 0:REACH] = p[:REACH]
        edge_out[slot, 1, x, REACH:] = q[:REACH]

    for x in range(X):
        p, q = p_in[0, x], q_in[0, x]
        field[1, 0, REACH + x, LEAD:LEAD + Y] = p
        field[1, 1, REACH + x, LEAD:LEAD + Y] = q
        put_edges(1, x, p, q)
        field[0, 0, REACH + x, LEAD:LEAD + Y] = pb_in[0, x]
        field[0, 1, REACH + x, LEAD:LEAD + Y] = qb_in[0, x]

    pl.semaphore_wait(barrier, 1 + sum(exists(*way).astype(jnp.int32) for way in WAYS + ((-1, 0), (1, 0))))
    for x in range(X):
        start_ready(1, x)

    for beyond, at in ((ix == 0, 0), (ix == nx - 1, X + REACH)):
        @pl.when(beyond)
        def _():
            tail[:, at:at + REACH] = jnp.zeros((2, REACH, Y, Z), jnp.float32)

            @pl.loop(1, STEPS + 2)
            def _(slot):
                field[slot, :, at:at + REACH, LEAD:LEAD + Y] = jnp.zeros((2, REACH, Y, Z), jnp.float32)
                edge_in[slot, :, at:at + REACH] = jnp.zeros((2, REACH, 8, Z), jnp.float32)
    for beyond, side in ((iy == 0, 0), (iy == ny - 1, 1)):
        @pl.when(beyond)
        def _():
            @pl.loop(1, STEPS + 2)
            def _(slot):
                edge_in[slot, side] = jnp.zeros((X + 2 * REACH, 8, Z), jnp.float32)

    for x in range(X):
        t, a, c = tilt[x], azimuth[x], courant[x]
        st, ct, sa, ca = jnp.sin(t), jnp.cos(t), jnp.sin(a), jnp.cos(a)
        square, double = st * st, 2.0 * st * ct
        weight[0, x] = square * ca * ca
        weight[1, x] = square * sa * sa
        weight[2, x] = ct * ct
        weight[3, x] = square * (2.0 * sa * ca)
        weight[4, x] = double * sa
        weight[5, x] = double * ca
        weight[6, x] = c * (1.0 + 2.0 * epsilon[x])
        weight[7, x] = c * (1.0 + 2.0 * delta[x])

    lane = lax.broadcasted_iota(jnp.int32, (Y, Z), 1)
    inside = {m: (lane + m >= 0) & (lane + m < Z) for m in range(-4, 5) if m}

    def along_z(value):
        def at(m):
            if m == 0:
                return value
            return jnp.where(inside[m], pltpu.roll(value, (-m) % Z, 1), 0.0)
        return at

    @pl.loop(1, STEPS + 1)
    def _(cur):
        def blend(f, i, x):
            w = weight[i, x]
            if f == 1:
                return w
            return 1.0 - w if i < 3 else -w

        for f in range(2):
            for x in range(X):
                value = field[cur, f, REACH + x, LEAD:LEAD + Y]
                partial[f, x] = blend(f, 2, x) * second_of(along_z(value))

        def open_edges(x):
            low, high = edge_in[cur, 0, x], edge_in[cur, 1, x]
            field[cur, 0, x, LEAD - REACH:LEAD] = low[REACH:]
            field[cur, 1, x, LEAD - REACH:LEAD] = low[:REACH]
            field[cur, 0, x, LEAD + Y:LEAD + Y + REACH] = high[:REACH]
            field[cur, 1, x, LEAD + Y:LEAD + Y + REACH] = high[REACH:]

        await_from(cur, (0, 1))
        for x in range(X):
            open_edges(REACH + x)
        for f in range(2):
            for x in range(X):
                def at_y(m):
                    return field[cur, f, REACH + x, LEAD + m:LEAD + m + Y]
                total = partial[f, x] + blend(f, 1, x) * second_of(at_y)
                partial[f, x] = total + blend(f, 4, x) * first_of(along_z(first_of(at_y)))

        await_from(cur, (2, 3, 4, 5, 6, 7))

        @pl.when(cur > 1)
        def _():
            share(cur).start()

        for x in range(REACH):
            open_edges(x)
            open_edges(X + REACH + x)
        for x in range(X):
            both = []
            for f in range(2):
                def at_x(m):
                    return field[cur, f, REACH + x + m, LEAD:LEAD + Y]

                def at_x_wide(m):
                    return field[cur, f, REACH + x + m, LEAD - REACH:LEAD + Y + REACH]
                total = partial[f, x] + blend(f, 0, x) * second_of(at_x)
                slope[f, x] = first_of(at_x_wide)
                total = total + blend(f, 5, x) * first_of(along_z(slope[f, x, REACH:REACH + Y]))
                both.append(total + blend(f, 3, x) * first_of(
                    lambda m: slope[f, x, REACH + m:REACH + m + Y]))
            h2p, h1q = both
            push = courant[x] * h1q
            p = 2.0 * field[cur, 0, REACH + x, LEAD:LEAD + Y] - field[cur - 1, 0, REACH + x, LEAD:LEAD + Y]
            q = 2.0 * field[cur, 1, REACH + x, LEAD:LEAD + Y] - field[cur - 1, 1, REACH + x, LEAD:LEAD + Y]
            p = p + (weight[6, x] * h2p + push)
            q = q + (weight[7, x] * h2p + push)
            field[cur + 1, 0, REACH + x, LEAD:LEAD + Y] = p
            field[cur + 1, 1, REACH + x, LEAD:LEAD + Y] = q
            put_edges(cur + 1, x, p, q)

            if (x + 1) % PIECE == 0 or x == X - 1 or (X - x - 1) % PIECE == 0:
                @pl.when(cur < STEPS)
                def _():
                    start_ready(cur + 1, x)

    for x in range(X):
        tail[0, REACH + x] = field[last, 0, REACH + x, LEAD:LEAD + Y]
    last_share().start()
    for cross in (True, False):
        for k in (2, 3):
            @pl.when(exists(*WAYS[k]))
            def _():
                last_copy(k, cross).start()
    for x in range(X):
        p_out[0, x] = field[last, 0, REACH + x, LEAD:LEAD + Y]
        q_out[0, x] = field[last, 1, REACH + x, LEAD:LEAD + Y]

    @pl.loop(2, STEPS + 1)
    def _(slot):
        share(slot).wait_recv()

    turn = 1 - 2 * sec
    half = Z // 2

    def term(i, x, j):
        shift = lags[i] * turn
        if j == plan.shape[0] - 1:
            return tail[0, REACH + x - shift] * tail[1, REACH + x + shift]
        slot = plan[j] + 1
        return field[slot, 0, REACH + x - shift, LEAD:LEAD + Y] * other[slot, REACH + x + shift]

    for i in range(lags.shape[0]):
        for x in range(X):
            total = term(i, x, 0)
            for j in range(1, plan.shape[0] - 1):
                total = total + term(i, x, j)
            stacked[i, x] = total

    @pl.loop(1, STEPS + 1)
    def _(slot):
        for k in range(len(WAYS)):
            @pl.when(exists(*WAYS[k]))
            def _():
                for c in pieces(k):
                    copy(slot, k, c).wait_send()

    @pl.loop(2, STEPS + 1)
    def _(slot):
        share(slot).wait_send()

    last_share().wait_recv()
    for cross in (True, False):
        for k in (2, 3):
            @pl.when(exists(-WAYS[k][0], 0))
            def _():
                last_copy(k, cross).wait_recv()
    for i in range(lags.shape[0]):
        for x in range(X):
            total = stacked[i, x] + term(i, x, plan.shape[0] - 1)
            image[i, x] = jnp.where(sec == 0, total, pltpu.roll(total, half, 1))[:, :half]
    for cross in (True, False):
        for k in (2, 3):
            @pl.when(exists(*WAYS[k]))
            def _():
                last_copy(k, cross).wait_send()
    last_share().wait_send()


def on_device(mesh_shape, *args):
    p, plan, lags = args[0], args[9], args[10]
    X, Y, Z = p.shape[1:]
    slots, wide = STEPS + 2, X + 2 * REACH
    dma = pltpu.SemaphoreType.DMA
    vmem, smem = pl.BlockSpec(memory_space=pltpu.VMEM), pl.BlockSpec(memory_space=pltpu.SMEM)
    return pl.pallas_call(
        functools.partial(kernel, mesh_shape),
        out_shape=(
            pltpu.VMEM(p.shape, jnp.float32),
            pltpu.VMEM(p.shape, jnp.float32),
            pltpu.VMEM((lags.shape[0], X, Y, Z // 2), jnp.float32),
        ),
        in_specs=[vmem] * 9 + [smem] * 2,
        out_specs=(vmem, vmem, vmem),
        scratch_shapes=[
            pltpu.VMEM((slots, 2, wide, Y + 2 * LEAD, Z), jnp.float32),
            pltpu.VMEM((slots, 2, X, 8, Z), jnp.float32),
            pltpu.VMEM((slots, 2, wide, 8, Z), jnp.float32),
            pltpu.VMEM((slots, wide, Y, Z), jnp.float32),
            pltpu.VMEM((8, X, Y, Z), jnp.float32),
            pltpu.VMEM((2, X, Y, Z), jnp.float32),
            pltpu.VMEM((2, X, Y + 2 * REACH, Z), jnp.float32),
            pltpu.VMEM((lags.shape[0], X, Y, Z), jnp.float32),
            pltpu.VMEM((2, wide, Y, Z), jnp.float32),
            dma((slots, len(WAYS), REACH // PIECE)),
            dma((slots, len(WAYS), REACH // PIECE)),
            dma((slots,)),
            dma((slots,)),
        ],
        compiler_params=pltpu.CompilerParams(collective_id=0, has_side_effects=True),
        name="steps",
    )(*args)


def solution(mesh):
    field, medium = P("sec", ("group", "gx"), "gy", None), P("gx", "gy", None)
    return jax.shard_map(
        functools.partial(on_device, (mesh.shape["gx"], mesh.shape["gy"])),
        mesh=mesh,
        in_specs=(field,) * 4 + (medium,) * 5 + (P(), P()),
        out_specs=(field, field, P(None, ("group", "gx"), "gy", "sec")),
        check_vma=False,
    )
```

```python
import functools

import jax
import jax.numpy as jnp
from jax import lax
from jax.experimental import pallas as pl
from jax.experimental.pallas import tpu as pltpu
from jax.sharding import PartitionSpec as P

STEPS = 8
REACH = 4
LEAD = 8
PIECE = 4

SECOND = (-205.0 / 72.0, 8.0 / 5.0, -1.0 / 5.0, 8.0 / 315.0, -1.0 / 560.0)
FIRST = (4.0 / 5.0, -1.0 / 5.0, 4.0 / 105.0, -1.0 / 280.0)
MESH = pl.DeviceIdType.MESH
WAYS = ((0, -1), (0, 1), (-1, 0), (1, 0), (-1, -1), (-1, 1), (1, -1), (1, 1))


def first_of(at):
    result = FIRST[0] * (at(1) - at(-1))
    for m in range(2, 5):
        result = result + FIRST[m - 1] * (at(m) - at(-m))
    return result


def second_of(at):
    result = SECOND[0] * at(0)
    for m in range(1, 5):
        result = result + SECOND[m] * (at(m) + at(-m))
    return result


def kernel(
    shape, p_in, pb_in, q_in, qb_in, courant, epsilon, delta, tilt, azimuth, plan, lags,
    p_out, q_out, image,
    field, edge_out, edge_in, other, weight, partial, slope, stacked, tail, send, recv, send_sec, recv_sec,
):
    nx, ny = shape
    ix, iy, sec = lax.axis_index("gx"), lax.axis_index("gy"), lax.axis_index("sec")
    X, Y, Z = p_in.shape[1:]
    rows = pl.ds(LEAD, Y)

    def exists(dx, dy):
        ok = (ix + dx >= 0) & (ix + dx < nx) & (iy + dy >= 0) & (iy + dy < ny)
        return ok

    def copy(slot, k, c):
        dx, dy = WAYS[k]
        begin, many = c * PIECE, PIECE
        if dx == 0:
            start, land, begin, many = 0, REACH, 0, X
        elif dx > 0:
            start, land = X - REACH, 0
        else:
            start, land = 0, X + REACH
        if dy == 0:
            src = field.at[slot, :, pl.ds(REACH + start + begin, many), rows, :]
            dst = field.at[slot, :, pl.ds(land + begin, many), rows, :]
        else:
            side = 0 if dy > 0 else 1
            src = edge_out.at[slot, side, pl.ds(start + begin, many)]
            dst = edge_in.at[slot, side, pl.ds(land + begin, many)]
        return pltpu.make_async_remote_copy(
            src_ref=src, dst_ref=dst, send_sem=send.at[slot, k, c], recv_sem=recv.at[slot, k, c],
            device_id={"gx": ix + dx, "gy": iy + dy}, device_id_type=MESH)

    def pieces(k):
        return range(REACH // PIECE if WAYS[k][0] else 1)

    last = STEPS + 1

    def last_copy(k, cross):
        dx = WAYS[k][0]
        start, land = (X, 0) if dx > 0 else (REACH, X + REACH)
        return pltpu.make_async_remote_copy(
            src_ref=tail.at[0, pl.ds(start, REACH)], dst_ref=tail.at[int(cross), pl.ds(land, REACH)],
            send_sem=send.at[last, k + 2 * cross, 0], recv_sem=recv.at[last, k + 2 * cross, 0],
            device_id={"gx": ix + dx, "sec": 1 - sec if cross else sec}, device_id_type=MESH)

    def share(slot):
        return pltpu.make_async_remote_copy(
            src_ref=field.at[slot, 0, :, rows, :], dst_ref=other.at[slot],
            send_sem=send_sec.at[slot], recv_sem=recv_sec.at[slot],
            device_id={"sec": 1 - sec}, device_id_type=MESH)

    def last_share():
        return pltpu.make_async_remote_copy(
            src_ref=tail.at[0, pl.ds(REACH, X)], dst_ref=tail.at[1, pl.ds(REACH, X)],
            send_sem=send_sec.at[last], recv_sem=recv_sec.at[last],
            device_id={"sec": 1 - sec}, device_id_type=MESH)

    def start_ready(slot, x):
        for k in (4, 5, 6, 7, 0, 1, 2, 3):
            dx = WAYS[k][0]
            for c in pieces(k):
                end = X - 1 if dx == 0 else (c + 1) * PIECE - 1 + (X - REACH if dx > 0 else 0)
                if end == x:
                    @pl.when(exists(*WAYS[k]))
                    def _():
                        copy(slot, k, c).start()

    def await_from(slot, ks):
        for k in ks:
            dx, dy = WAYS[k]

            @pl.when(exists(-dx, -dy))
            def _():
                for c in pieces(k):
                    copy(slot, k, c).wait_recv()

    barrier = pltpu.get_barrier_semaphore()
    for dx, dy in WAYS:
        @pl.when(exists(dx, dy))
        def _():
            pl.semaphore_signal(barrier, inc=1, device_id={"gx": ix + dx, "gy": iy + dy}, device_id_type=MESH)
    for dx in (-1, 1):
        @pl.when(exists(dx, 0))
        def _():
            pl.semaphore_signal(barrier, inc=1, device_id={"gx": ix + dx, "sec": 1 - sec}, device_id_type=MESH)
    pl.semaphore_signal(barrier, inc=1, device_id={"sec": 1 - sec}, device_id_type=MESH)

    def put_edges(slot, x, p, q):
        edge_out[slot, 0, x, 0:REACH] = q[Y - REACH:]
        edge_out[slot, 0, x, REACH:] = p[Y - REACH:]
        edge_out[slot, 1, x, 0:REACH] = p[:REACH]
        edge_out[slot, 1, x, REACH:] = q[:REACH]

    for x in range(X):
        p, q = p_in[0, x], q_in[0, x]
        field[1, 0, REACH + x, LEAD:LEAD + Y] = p
        field[1, 1, REACH + x, LEAD:LEAD + Y] = q
        put_edges(1, x, p, q)
        field[0, 0, REACH + x, LEAD:LEAD + Y] = pb_in[0, x]
        field[0, 1, REACH + x, LEAD:LEAD + Y] = qb_in[0, x]

    pl.semaphore_wait(barrier, 1 + sum(exists(*way).astype(jnp.int32) for way in WAYS + ((-1, 0), (1, 0))))
    for x in range(X):
        start_ready(1, x)

    for beyond, at in ((ix == 0, 0), (ix == nx - 1, X + REACH)):
        @pl.when(beyond)
        def _():
            tail[:, at:at + REACH] = jnp.zeros((2, REACH, Y, Z), jnp.float32)

            @pl.loop(1, STEPS + 2)
            def _(slot):
                field[slot, :, at:at + REACH, LEAD:LEAD + Y] = jnp.zeros((2, REACH, Y, Z), jnp.float32)
                edge_in[slot, :, at:at + REACH] = jnp.zeros((2, REACH, 8, Z), jnp.float32)
    for beyond, side in ((iy == 0, 0), (iy == ny - 1, 1)):
        @pl.when(beyond)
        def _():
            @pl.loop(1, STEPS + 2)
            def _(slot):
                edge_in[slot, side] = jnp.zeros((X + 2 * REACH, 8, Z), jnp.float32)

    for x in range(X):
        t, a, c = tilt[x], azimuth[x], courant[x]
        st, ct, sa, ca = jnp.sin(t), jnp.cos(t), jnp.sin(a), jnp.cos(a)
        square, double = st * st, 2.0 * st * ct
        weight[0, x] = square * ca * ca
        weight[1, x] = square * sa * sa
        weight[2, x] = ct * ct
        weight[3, x] = square * (2.0 * sa * ca)
        weight[4, x] = double * sa
        weight[5, x] = double * ca
        weight[6, x] = c * (1.0 + 2.0 * epsilon[x])
        weight[7, x] = c * (1.0 + 2.0 * delta[x])

    lane = lax.broadcasted_iota(jnp.int32, (Y, Z), 1)
    inside = {m: (lane + m >= 0) & (lane + m < Z) for m in range(-4, 5) if m}

    def along_z(value):
        def at(m):
            if m == 0:
                return value
            return jnp.where(inside[m], pltpu.roll(value, (-m) % Z, 1), 0.0)
        return at

    @pl.loop(1, STEPS + 1)
    def _(cur):
        def blend(f, i, x):
            w = weight[i, x]
            if f == 1:
                return w
            return 1.0 - w if i < 3 else -w

        for f in range(2):
            for x in range(X):
                value = field[cur, f, REACH + x, LEAD:LEAD + Y]
                partial[f, x] = blend(f, 2, x) * second_of(along_z(value))

        def open_edges(x):
            low, high = edge_in[cur, 0, x], edge_in[cur, 1, x]
            field[cur, 0, x, LEAD - REACH:LEAD] = low[REACH:]
            field[cur, 1, x, LEAD - REACH:LEAD] = low[:REACH]
            field[cur, 0, x, LEAD + Y:LEAD + Y + REACH] = high[:REACH]
            field[cur, 1, x, LEAD + Y:LEAD + Y + REACH] = high[REACH:]

        await_from(cur, (0, 1))
        for x in range(X):
            open_edges(REACH + x)
        for f in range(2):
            for x in range(X):
                def at_y(m):
                    return field[cur, f, REACH + x, LEAD + m:LEAD + m + Y]
                total = partial[f, x] + blend(f, 1, x) * second_of(at_y)
                partial[f, x] = total + blend(f, 4, x) * first_of(along_z(first_of(at_y)))

        await_from(cur, (4, 5, 6, 7))
        for x in range(REACH):
            open_edges(x)
            open_edges(X + REACH + x)
        await_from(cur, (2, 3))

        @pl.when(cur > 1)
        def _():
            share(cur).start()

        for x in range(X):
            both = []
            for f in range(2):
                def at_x(m):
                    return field[cur, f, REACH + x + m, LEAD:LEAD + Y]

                def at_x_wide(m):
                    return field[cur, f, REACH + x + m, LEAD - REACH:LEAD + Y + REACH]
                total = partial[f, x] + blend(f, 0, x) * second_of(at_x)
                slope[f, x] = first_of(at_x_wide)
                total = total + blend(f, 5, x) * first_of(along_z(slope[f, x, REACH:REACH + Y]))
                both.append(total + blend(f, 3, x) * first_of(
                    lambda m: slope[f, x, REACH + m:REACH + m + Y]))
            h2p, h1q = both
            push = courant[x] * h1q
            p = 2.0 * field[cur, 0, REACH + x, LEAD:LEAD + Y] - field[cur - 1, 0, REACH + x, LEAD:LEAD + Y]
            q = 2.0 * field[cur, 1, REACH + x, LEAD:LEAD + Y] - field[cur - 1, 1, REACH + x, LEAD:LEAD + Y]
            p = p + (weight[6, x] * h2p + push)
            q = q + (weight[7, x] * h2p + push)
            field[cur + 1, 0, REACH + x, LEAD:LEAD + Y] = p
            field[cur + 1, 1, REACH + x, LEAD:LEAD + Y] = q
            put_edges(cur + 1, x, p, q)

            if (x + 1) % PIECE == 0 or x == X - 1 or (X - x - 1) % PIECE == 0:
                @pl.when(cur < STEPS)
                def _():
                    start_ready(cur + 1, x)

    for x in range(X):
        tail[0, REACH + x] = field[last, 0, REACH + x, LEAD:LEAD + Y]
    last_share().start()
    for cross in (True, False):
        for k in (2, 3):
            @pl.when(exists(*WAYS[k]))
            def _():
                last_copy(k, cross).start()
    for x in range(X):
        p_out[0, x] = field[last, 0, REACH + x, LEAD:LEAD + Y]
        q_out[0, x] = field[last, 1, REACH + x, LEAD:LEAD + Y]

    @pl.loop(2, STEPS + 1)
    def _(slot):
        share(slot).wait_recv()

    turn = 1 - 2 * sec
    half = Z // 2

    def term(i, x, j):
        shift = lags[i] * turn
        if j == plan.shape[0] - 1:
            return tail[0, REACH + x - shift] * tail[1, REACH + x + shift]
        slot = plan[j] + 1
        return field[slot, 0, REACH + x - shift, LEAD:LEAD + Y] * other[slot, REACH + x + shift]

    for i in range(lags.shape[0]):
        for x in range(X):
            total = term(i, x, 0)
            for j in range(1, plan.shape[0] - 1):
                total = total + term(i, x, j)
            stacked[i, x] = total

    @pl.loop(1, STEPS + 1)
    def _(slot):
        for k in range(len(WAYS)):
            @pl.when(exists(*WAYS[k]))
            def _():
                for c in pieces(k):
                    copy(slot, k, c).wait_send()

    @pl.loop(2, STEPS + 1)
    def _(slot):
        share(slot).wait_send()

    last_share().wait_recv()
    for cross in (True, False):
        for k in (2, 3):
            @pl.when(exists(-WAYS[k][0], 0))
            def _():
                last_copy(k, cross).wait_recv()
    for i in range(lags.shape[0]):
        for x in range(X):
            total = stacked[i, x] + term(i, x, plan.shape[0] - 1)
            image[i, x] = jnp.where(sec == 0, total, pltpu.roll(total, half, 1))[:, :half]
    for cross in (True, False):
        for k in (2, 3):
            @pl.when(exists(*WAYS[k]))
            def _():
                last_copy(k, cross).wait_send()
    last_share().wait_send()


def on_device(mesh_shape, *args):
    p, plan, lags = args[0], args[9], args[10]
    X, Y, Z = p.shape[1:]
    slots, wide = STEPS + 2, X + 2 * REACH
    dma = pltpu.SemaphoreType.DMA
    vmem, smem = pl.BlockSpec(memory_space=pltpu.VMEM), pl.BlockSpec(memory_space=pltpu.SMEM)
    return pl.pallas_call(
        functools.partial(kernel, mesh_shape),
        out_shape=(
            pltpu.VMEM(p.shape, jnp.float32),
            pltpu.VMEM(p.shape, jnp.float32),
            pltpu.VMEM((lags.shape[0], X, Y, Z // 2), jnp.float32),
        ),
        in_specs=[vmem] * 9 + [smem] * 2,
        out_specs=(vmem, vmem, vmem),
        scratch_shapes=[
            pltpu.VMEM((slots, 2, wide, Y + 2 * LEAD, Z), jnp.float32),
            pltpu.VMEM((slots, 2, X, 8, Z), jnp.float32),
            pltpu.VMEM((slots, 2, wide, 8, Z), jnp.float32),
            pltpu.VMEM((slots, wide, Y, Z), jnp.float32),
            pltpu.VMEM((8, X, Y, Z), jnp.float32),
            pltpu.VMEM((2, X, Y, Z), jnp.float32),
            pltpu.VMEM((2, X, Y + 2 * REACH, Z), jnp.float32),
            pltpu.VMEM((lags.shape[0], X, Y, Z), jnp.float32),
            pltpu.VMEM((2, wide, Y, Z), jnp.float32),
            dma((slots, len(WAYS), REACH // PIECE)),
            dma((slots, len(WAYS), REACH // PIECE)),
            dma((slots,)),
            dma((slots,)),
        ],
        compiler_params=pltpu.CompilerParams(collective_id=0, has_side_effects=True),
        name="steps",
    )(*args)


def solution(mesh):
    field, medium = P("sec", ("group", "gx"), "gy", None), P("gx", "gy", None)
    return jax.shard_map(
        functools.partial(on_device, (mesh.shape["gx"], mesh.shape["gy"])),
        mesh=mesh,
        in_specs=(field,) * 4 + (medium,) * 5 + (P(), P()),
        out_specs=(field, field, P(None, ("group", "gx"), "gy", "sec")),
        check_vma=False,
    )
```
